32 devices in a mesh: cuts: 2 (over core), lx: 2 (over x), ly: 8 (over z, y).
Axes of the slice: x: 2, y: 2, z: 4, core: 2. Of those that a mesh axis runs over, the one named last changes fastest.
Arguments:
- disorder: int32 [16, 16, 128], P('lx', 'ly'), may hold values from 0 to 255
- slice_bounds: float32 [12, 2], P('cuts'), may hold values from -1.5 to 1.5
- start: float32 [12, 32, 16, 16, 128], P('cuts', None, 'lx', 'ly'), may hold values from -36 to 36
- ritz: float32 [12, 8, 16, 16, 128], P('cuts', None, 'lx', 'ly'), may hold values from -4 to 4
Outputs:
- block: float32 [12, 32, 16, 16, 128], P('cuts', None, 'lx', 'ly')
- correlations: float32 [12, 16, 32], P('cuts')
The draws below stay inside these ranges and needn't reach their ends.
All inputs are finite; a program needn't handle non-finite values.
Results may differ from the reference program's by a relative error of at most 0.000096.
Values sent between devices are 32-bit elements; how exact they have to be, the bound alone decides.
A program may use at most 64 MiB of HBM per device.

```python
import jax
import jax.numpy as jnp
from jax import lax

NV = 32
RITZ = 8
DEG = 2
LEVELS = 256
NZ = 128
SLICES = 12
NX = 16
NY = 16


def ritz_field(key):
    shape = (SLICES, RITZ, NX, NY, NZ)
    values = jnp.clip(jax.random.normal(jax.random.fold_in(key, 7), shape, jnp.float32), -4.0, 4.0)
    return values


def draw_ritz(key, part):
    return ritz_field(key)


def draw_start(key, part):
    ritz_all = ritz_field(key)
    empty = jnp.zeros((1, RITZ, NX, NY, NZ), jnp.float32)
    lower = jnp.concatenate([empty, ritz_all[:-1]], 0)
    upper = jnp.concatenate([ritz_all[1:], empty], 0)
    window = jnp.concatenate([lower, upper], 1)
    shape = (SLICES, NV, NX, NY, NZ)
    noise = jnp.clip(jax.random.normal(jax.random.fold_in(key, 11), shape, jnp.float32), -4.0, 4.0)
    weights = jax.random.uniform(jax.random.fold_in(key, 13), (SLICES, NV, 2 * RITZ), jnp.float32, -1.0, 1.0)

    def drawn_slice(items):
        window_one = items[0]
        weight_one = items[1]
        planted = jnp.zeros((NV, NX, NY, NZ), jnp.float32)
        for column in range(2 * RITZ):
            planted = planted + weight_one[:, column][:, None, None, None] * window_one[column][None]
        return planted
    planted_all = lax.map(drawn_slice, (window, weights))
    return noise + 0.5 * planted_all


def set_ends(entries, rng, low, largest):
    shape = entries.shape
    spot = [jax.random.randint(jax.random.fold_in(rng, axis), (), 0, shape[axis]) for axis in range(len(shape))]
    entries = entries.at[tuple(spot)].set(low)
    longest = shape.index(max(shape))
    spot[longest] = (spot[longest] + 1) % shape[longest]
    return entries.at[tuple(spot)].set(largest)


def steps_of(stream_key, extent, shards, least, top_value):
    def one(axis_at, blocks):
        draws = jax.random.uniform(jax.random.fold_in(jax.random.fold_in(stream_key, 6), axis_at), (blocks,), jnp.float32, least / len(shards), top_value / len(shards))
        return jnp.repeat(jnp.exp(draws), extent[axis_at] // blocks).reshape((-1,) + (1,) * (len(extent) - axis_at - 1))

    level = one(*shards[0])
    for cut in shards[1:]:
        level = level * one(*cut)
    return level


def setup_inputs(seed: int = 0) -> dict:
    streams_of = jax.random.split(jax.random.key(seed), 5)
    return {
        "disorder": set_ends(jax.random.randint(streams_of[0], (NX, NY, NZ), 0, LEVELS), jax.random.fold_in(streams_of[0], 1), 0, LEVELS - 1).astype(jnp.int32),
        "slice_bounds": jnp.clip(jax.random.uniform(streams_of[1], (SLICES, 2), jnp.float32, -1.5, 1.5) * steps_of(streams_of[1], (SLICES, 2), ((0, 2),), -0.4, 0.0), -1.5, 1.5),
        "start": draw_start(jax.random.fold_in(streams_of[4], 71), 0),
        "ritz": draw_ritz(jax.random.fold_in(streams_of[4], 71), 0),
    }


def scaled_operator(field, onsite, centre):
    beside = jnp.roll(field, 1, 1) + jnp.roll(field, -1, 1)
    beside = beside + jnp.roll(field, 1, 2) + jnp.roll(field, -1, 2)
    beside = beside + jnp.roll(field, 1, 3) + jnp.roll(field, -1, 3)
    return ((onsite[None] - centre) * field - beside) / 16.0

def one_slice(onsite, bounds, vectors, lower, upper):
    centre = (bounds[0] + bounds[1]) / 2.0
    previous = vectors
    current = scaled_operator(vectors, onsite, centre)
    for step in range(DEG - 1):
        previous, current = (current, 2.0 * scaled_operator(current, onsite, centre) - previous)
    cells = NX * NY * NZ
    hp = lax.Precision.HIGHEST
    filtered = current.reshape(NV, cells)
    window = jnp.concatenate([lower, upper], 0).reshape(2 * RITZ, cells)
    correlation = jnp.einsum('rc,vc->rv', window, filtered, precision=hp) / jnp.float32(cells)
    cleaned = filtered - jnp.einsum('rv,rc->vc', correlation, window, precision=hp)
    gram = jnp.einsum('ac,bc->ab', cleaned, cleaned, precision=hp) / jnp.float32(cells)
    factor = jnp.linalg.cholesky(gram)
    result = jax.scipy.linalg.solve_triangular(factor, cleaned, lower=True)
    return (result.reshape(NV, NX, NY, NZ), correlation)

def reference(disorder, slice_bounds, start, ritz):
    onsite = 16.5 * (disorder.astype(jnp.float32) / jnp.float32(LEVELS - 1) - 0.5)
    empty = jnp.zeros((1, RITZ, NX, NY, NZ), jnp.float32)
    lower = jnp.concatenate([empty, ritz[:-1]], 0)
    upper = jnp.concatenate([ritz[1:], empty], 0)

    def run(items):
        return one_slice(onsite, items[0], items[1], items[2], items[3])
    block, correlations = lax.map(run, (slice_bounds, start, lower, upper))
    return (block, correlations)
```

```python
import functools

import jax
import jax.numpy as jnp
from jax import lax
from jax.experimental import pallas as pl
from jax.experimental.pallas import tpu as pltpu
from jax.sharding import PartitionSpec as P

LEVELS = 256
MESH = pl.DeviceIdType.MESH
HP = lax.Precision.HIGHEST
H = 2


def kernel(dims, dis, bnd, start, ritz, out, cor, E, T, O, U, FA, FT, RA, ACC, LM, PK, RX, RZ, SM, AL,
           hs, hr, fs, fr, rs, rr, xs, xr, zs, zr, gs, gr):
    nc, nx, ny, count, NV, NR, X, Y, NZ = dims
    S = count // 2
    R = 2 * Y
    J = X * Y
    K = ny // 2
    ng = nx * 2
    tg = RX.shape[1]
    tiles = ng * tg
    total = float(J * NZ * nx * ny)
    cut, mx, my = lax.axis_index("cuts"), lax.axis_index("lx"), lax.axis_index("ly")
    p = lax.rem(my, 2)
    q = 1 - p
    kz = my // 2
    g = mx * 2 + p
    partner = kz * 2 + q
    zup = lax.rem(kz + 1, K) * 2 + p
    zdown = lax.rem(kz + K - 1, K) * 2 + p
    xup = lax.rem(mx + 1, nx)
    xdown = lax.rem(mx + nx - 1, nx)

    barrier = pltpu.get_barrier_semaphore()

    def greet(dev):
        pl.semaphore_signal(barrier, inc=1, device_id=dev, device_id_type=MESH)

    def in_plane(o):
        t = lax.rem(g + o, ng)
        return t, (cut, t // 2, kz * 2 + lax.rem(t, 2))

    def in_line(o):
        t = lax.rem(kz + o, K)
        return t, (cut, mx, t * 2 + p)

    for o in range(1, ng):
        greet(in_plane(o)[1])
    for o in range(1, K):
        greet(in_line(o)[1])
    cup = (lax.rem(cut + 1, nc), mx, my)
    cdown = (lax.rem(cut + nc - 1, nc), mx, my)
    greet(cup)
    greet(cdown)

    lo = H + Y * p
    for x in range(X):
        for r in range(Y):
            row = dis[pl.ds(x * Y + r, 1), :].astype(jnp.float32)
            row = 16.5 * (row / jnp.float32(LEVELS - 1) - 0.5)
            O[H + x, lo + r] = jnp.broadcast_to(row, (8, NZ))
    for c in range(S):
        for x in range(X):
            for r in range(Y):
                pick = pl.ds(x * Y + r, NV, stride=J)
                T[c, x, r] = start[q * S + c, pick, :]
                E[c, H + x, lo + r] = start[p * S + c, pick, :]
    for s in range(count):
        for x in range(X):
            for r in range(Y):
                RA[s + 1, x, r] = ritz[s, pl.ds(x * Y + r, NR, stride=J), :]
    pl.semaphore_wait(barrier, ng + K)

    pending = []

    def send(src, dst, ss, rs_, dev):
        copy = pltpu.make_async_remote_copy(
            src_ref=src, dst_ref=dst, send_sem=ss, recv_sem=rs_, device_id=dev, device_id_type=MESH)
        copy.start()
        pending.append(copy)

    def arrived(dst, rs_):
        pltpu.make_async_remote_copy(
            src_ref=dst, dst_ref=dst, send_sem=rs_, recv_sem=rs_,
            device_id=(cut, mx, partner), device_id_type=MESH).wait_recv()

    fields = [(S, O)] + [(c, E.at[c]) for c in range(S)]
    xi = pl.ds(H, X)
    xy = (cut, mx, partner)

    def row_block(at):
        return pl.ds(at, Y)

    def send_rows(c, buf, half):
        up = half
        target = jnp.where(up == 1, zup, zdown)
        dst_row = jnp.where(up == 1, 0, H + R)
        side = 1 - up
        send(buf.at[xi, row_block(H + Y * half)], buf.at[xi, row_block(dst_row)],
             hs.at[c, 1 + side], hr.at[c, 1 + side], (cut, mx, target))

    for c, buf in fields:
        src = buf.at[xi, row_block(lo)] if c == S else T.at[c]
        send(src, buf.at[xi, row_block(lo)], hs.at[c, 0], hr.at[c, 0], xy)
    for c, buf in fields:
        send_rows(c, buf, p)
    send(RA.at[count], RA.at[0], rs.at[0], rr.at[0], cup)
    send(RA.at[1], RA.at[count + 1], rs.at[1], rr.at[1], cdown)

    own = pl.ds(H, R)
    for c, buf in fields:
        arrived(buf.at[xi, row_block(H + Y * q)], hr.at[c, 0])
        send_rows(c, buf, q)
        send(buf.at[pl.ds(X, H), own], buf.at[pl.ds(0, H), own], hs.at[c, 3], hr.at[c, 3], (cut, xup, my))
        send(buf.at[pl.ds(H, H), own], buf.at[pl.ds(H + X, H), own], hs.at[c, 4], hr.at[c, 4], (cut, xdown, my))

    def point(src, c, x, r, centre):
        v = src(x, r)
        beside = src(x + 1, r) + src(x - 1, r)
        beside = beside + src(x, r + 1) + src(x, r - 1)
        beside = beside + pltpu.roll(v, 1, 1) + pltpu.roll(v, NZ - 1, 1)
        level = O[x, r] - centre
        level = jnp.concatenate([level] * (NV // 8), 0)
        return (level * v - beside) * 0.0625

    for c, buf in fields:
        for side, row in ((0, 0), (1, H + R)):
            arrived(buf.at[xi, row_block(row)], hr.at[c, 1 + side])
        for side, row in ((0, 1), (1, H + R)):
            send(buf.at[H + X - 1, row], buf.at[1, row], hs.at[c, 5 + 2 * side], hr.at[c, 5 + 2 * side], (cut, xup, my))
            send(buf.at[H, row], buf.at[H + X, row], hs.at[c, 6 + 2 * side], hr.at[c, 6 + 2 * side], (cut, xdown, my))
        arrived(buf.at[pl.ds(0, H), own], hr.at[c, 3])
        arrived(buf.at[pl.ds(H + X, H), own], hr.at[c, 4])
        for side, row in ((0, 1), (1, H + R)):
            arrived(buf.at[1, row], hr.at[c, 5 + 2 * side])
            arrived(buf.at[H + X, row], hr.at[c, 6 + 2 * side])
        if c == S:
            continue
        s = p * S + c
        centre = (bnd[s, 0] + bnd[s, 1]) / 2.0

        def from_e(x, r, c=c):
            return E[c, x, r]

        def from_u(x, r):
            return U[x, r]

        for x in (1, H + X):
            for r in range(H, H + R):
                U[x, r] = point(from_e, c, x, r, centre)

        def first(i, carry, c=c, centre=centre):
            for r in range(1, H + R + 1):
                U[H + i, r] = point(from_e, c, H + i, r, centre)
            return carry

        lax.fori_loop(0, X, first, 0)

        def second(i, carry, c=c, s=s, centre=centre):
            for r in range(Y):
                a = H + Y * p + r
                FA[s, i, r] = 2.0 * point(from_u, c, H + i, a, centre) - E[c, H + i, a]
                b = H + Y * q + r
                FT[c, i, r] = 2.0 * point(from_u, c, H + i, b, centre) - E[c, H + i, b]
            return carry

        lax.fori_loop(0, X, second, 0)
        send(FT.at[c], FA.at[s], fs.at[c], fr.at[c], xy)

    arrived(RA.at[0], rr.at[0])
    arrived(RA.at[count + 1], rr.at[1])

    @pl.when(cut == 0)
    def _():
        RA[0] = jnp.zeros((X, Y, NR, NZ), jnp.float32)

    @pl.when(cut == nc - 1)
    def _():
        RA[count + 1] = jnp.zeros((X, Y, NR, NZ), jnp.float32)

    for c in range(S):
        arrived(FA.at[q * S + c], fr.at[c])

    contract = (((1,), (1,)), ((), ()))
    ACC[...] = jnp.zeros(ACC.shape, jnp.float32)

    def grams(i, carry):
        z = [jnp.concatenate([FA[s, i, r] for s in range(count)] + [RA[t, i, r] for t in range(count + 2)], 0)
             for r in range(Y)]
        z = jnp.concatenate(z, 1)
        ACC[...] += lax.dot_general(z, z, contract, precision=HP, preferred_element_type=jnp.float32)
        return carry

    lax.fori_loop(0, X, grams, 0)

    NL = ACC.shape[1]
    base = count * NV
    lane = lax.broadcasted_iota(jnp.int32, (8, NL), 1)

    def masked(row, first, width):
        keep = jnp.logical_and(lane >= first, lane < first + width)
        return jnp.where(keep, ACC[pl.ds(row, 8), :], 0.0)

    packed = []
    for b in range(NV // 8):
        acc = jnp.zeros((8, NL), jnp.float32)
        for s in range(count):
            acc = acc + masked(s * NV + b * 8, s * NV, NV)
        if b == 0:
            for t in range(count + 2):
                acc = acc + masked(base + t * NR, base + t * NR, NR)
        if b == 1:
            for s in range(count):
                acc = acc + masked(base + s * NR, base + (s + 2) * NR, NR)
        if b == 2:
            for s in range(count):
                acc = acc + masked(base + (s + 2) * NR, base + s * NR, NR)
        packed.append(acc)
    for b in range(2):
        acc = jnp.zeros((8, NL), jnp.float32)
        for s in range(count):
            acc = acc + masked(base + (s + 2 * b) * NR, s * NV, NV)
        packed.append(acc)
    halves = NL // 128
    used = len(packed) * halves
    for i in range(tiles):
        if i < used:
            h = i % halves
            PK[i] = packed[i // halves][:, h * 128:(h + 1) * 128]
        else:
            PK[i] = jnp.zeros((8, 128), jnp.float32)

    RX[g] = PK[pl.ds(g * tg, tg)]
    for o in range(1, ng):
        t, dev = in_plane(o)
        send(PK.at[pl.ds(t * tg, tg)], RX.at[g], xs.at[o], xr.at[g], dev)
    for o in range(1, ng):
        t, _ = in_plane(o)
        arrived(RX.at[t], xr.at[t])
    mine = RX[0]
    for t in range(1, ng):
        mine = mine + RX[t]
    RZ[kz] = mine
    SM[...] = mine
    for o in range(1, K):
        t, dev = in_line(o)
        send(SM, RZ.at[kz], zs.at[o], zr.at[kz], dev)
    for o in range(1, K):
        t, _ = in_line(o)
        arrived(RZ.at[t], zr.at[t])
    mine = RZ[0]
    for t in range(1, K):
        mine = mine + RZ[t]
    AL[g] = mine
    for o in range(1, ng):
        t, dev = in_plane(o)
        send(AL.at[g], AL.at[g], gs.at[o], gr.at[g], dev)
    for o in range(1, ng):
        t, _ = in_plane(o)
        arrived(AL.at[t], gr.at[t])

    def tile(row, first):
        i = row * halves + first // 128
        value = AL[i // tg, i % tg] * (1.0 / total)
        shift = first % 128
        return pltpu.roll(value, 128 - shift, 1) if shift else value

    l8 = lax.broadcasted_iota(jnp.int32, (8, 128), 1)
    l32 = lax.broadcasted_iota(jnp.int32, (NV, 128), 1)
    r32 = lax.broadcasted_iota(jnp.int32, (NV, 128), 0)
    eye = jnp.where(l32 == r32 + NV, 1.0, 0.0)
    e16r = lax.broadcasted_iota(jnp.int32, (2 * NR, 128), 0)
    e16l = lax.broadcasted_iota(jnp.int32, (2 * NR, 128), 1)
    corrs, mats = [], []
    for s in range(count):
        corr = jnp.concatenate([tile(NV // 8 + b, s * NV) for b in range(2)], 0)[:, :NV]
        corrs.append(corr)
        cor[s] = corr
        a00 = tile(0, base + s * NR)
        a11 = pltpu.roll(tile(0, base + (s + 2) * NR), NR, 1)
        a01 = pltpu.roll(tile(1, base + (s + 2) * NR), NR, 1)
        a10 = tile(2, base + s * NR)
        b = jnp.concatenate([jnp.where(l8 < NR, a00, a01), jnp.where(l8 < NR, a10, a11)], 0)
        b = jnp.where(e16r == e16l, 2.0, 0.0) - b
        b = b[:, :2 * NR]
        bc = lax.dot_general(b, corr, (((1,), (0,)), ((), ())), precision=HP, preferred_element_type=jnp.float32)
        sub = lax.dot_general(corr, bc, (((0,), (0,)), ((), ())), precision=HP, preferred_element_type=jnp.float32)
        ff = jnp.concatenate([tile(b_, s * NV) for b_ in range(NV // 8)], 0)
        sub = jnp.concatenate([sub, jnp.zeros((NV, 128 - NV), jnp.float32)], 1)
        mats.append(jnp.where(l32 < NV, ff - sub, eye)[None])
    M = jnp.concatenate(mats, 0)
    rows = lax.broadcasted_iota(jnp.int32, (1, NV, 1), 1)
    for k in range(NV):
        pivot = M[:, k:k + 1, :]
        inv = 1.0 / pivot[:, :, k:k + 1]
        f = jnp.where(rows > k, M[:, :, k:k + 1] * inv, 0.0)
        M = M - f * pivot
    diag = jnp.sum(jnp.where(l32[None] == r32[None], M, 0.0), axis=2, keepdims=True)
    M = M * (1.0 / jnp.sqrt(diag))
    ident = jnp.where(l32 == r32, 1.0, 0.0)[:, :NV]
    for s in range(count):
        linv = pltpu.roll(M[s], 128 - NV, 1)[:, :NV]
        full = jnp.concatenate([ident, -corrs[s]], 0)
        LM[s] = lax.dot_general(linv, full, contract, precision=HP, preferred_element_type=jnp.float32)

    def finish(s, carry):
        left = LM[s]
        for x in range(X):
            z = [jnp.concatenate([FA[s, x, r], RA[s, x, r], RA[s + 2, x, r]], 0) for r in range(Y)]
            z = jnp.concatenate(z, 1)
            o = lax.dot_general(left, z, (((1,), (0,)), ((), ())), precision=HP, preferred_element_type=jnp.float32)
            for r in range(Y):
                out[s, pl.ds(x * Y + r, NV, stride=J), :] = o[:, r * NZ:(r + 1) * NZ]
        return carry

    lax.fori_loop(0, count, finish, 0)
    for copy in pending:
        copy.wait_send()


def on_device(disorder, slice_bounds, start, ritz):
    nc, nx, ny = (lax.axis_size(a) for a in ("cuts", "lx", "ly"))
    count, NV, X, Y, NZ = start.shape
    NR = ritz.shape[1]
    J = X * Y
    S, R, K, ng = count // 2, 2 * Y, ny // 2, nx * 2
    NL = count * NV + (count + 2) * NR
    tg = -(-((NV + 2 * NR) // 8 * (NL // 128)) // ng)
    f32 = jnp.float32
    V = pltpu.VMEM
    D = pltpu.SemaphoreType.DMA
    dims = (nc, nx, ny, count, NV, NR, X, Y, NZ)
    vm = pl.BlockSpec(memory_space=pltpu.VMEM)
    block, corr = pl.pallas_call(
        functools.partial(kernel, dims),
        out_shape=(jax.ShapeDtypeStruct((count, NV * J, NZ), f32),
                   jax.ShapeDtypeStruct((count, 2 * NR, NV), f32)),
        in_specs=[vm, pl.BlockSpec(memory_space=pltpu.SMEM), vm, vm],
        out_specs=(vm, vm),
        scratch_shapes=[
            V((S, X + 2 * H, R + 2 * H, NV, NZ), f32),
            V((S, X, Y, NV, NZ), f32),
            V((X + 2 * H, R + 2 * H, 8, NZ), f32),
            V((X + 2 * H, R + 2 * H, NV, NZ), f32),
            V((count, X, Y, NV, NZ), f32),
            V((S, X, Y, NV, NZ), f32),
            V((count + 2, X, Y, NR, NZ), f32),
            V((NL, NL), f32),
            V((count, NV, NV + 2 * NR), f32),
            V((ng * tg, 8, 128), f32),
            V((ng, tg, 8, 128), f32),
            V((K, tg, 8, 128), f32),
            V((tg, 8, 128), f32),
            V((ng, tg, 8, 128), f32),
            D((S + 1, 9)), D((S + 1, 9)), D((S,)), D((S,)), D((2,)), D((2,)),
            D((ng,)), D((ng,)), D((K,)), D((K,)), D((ng,)), D((ng,)),
        ],
        compiler_params=pltpu.CompilerParams(collective_id=0, has_side_effects=True, vmem_limit_bytes=48 << 20),
    )(disorder.reshape(J, NZ), slice_bounds, start.reshape(count, NV * J, NZ), ritz.reshape(count, NR * J, NZ))
    return (block.reshape(start.shape), corr)


def solution(mesh):
    in_specs = (
        P("lx", "ly", None),
        P("cuts", None),
        P("cuts", None, "lx", "ly", None),
        P("cuts", None, "lx", "ly", None),
    )
    out_specs = (P("cuts", None, "lx", "ly", None), P("cuts", None, None))
    return jax.shard_map(
        on_device, mesh=mesh, in_specs=in_specs, out_specs=out_specs, check_vma=False
    )
```

```python
import functools

import jax
import jax.numpy as jnp
from jax import lax
from jax.experimental import pallas as pl
from jax.experimental.pallas import tpu as pltpu
from jax.sharding import PartitionSpec as P

LEVELS = 256
MESH = pl.DeviceIdType.MESH
HP = lax.Precision.HIGHEST
H = 2


def kernel(dims, dis_h, bnd, start_h, ritz_h, out, cor, dis, start, ritz, ls, E, T, O, U, FA, FT, RA, ACC, LM, PK, RX, RZ, SM, AL,
           hs, hr, fs, fr, rs, rr, xs, xr, zs, zr, gs, gr):
    nc, nx, ny, count, NV, NR, X, Y, NZ = dims
    S = count // 2
    CH = E.shape[0] // S
    NC = S * CH
    W = NV // CH
    R = 2 * Y
    J = X * Y
    K = ny // 2
    ng = nx * 2
    tg = RX.shape[1]
    tiles = ng * tg
    total = float(J * NZ * nx * ny)
    cut, mx, my = lax.axis_index("cuts"), lax.axis_index("lx"), lax.axis_index("ly")
    p = lax.rem(my, 2)
    q = 1 - p
    kz = my // 2
    g = mx * 2 + p
    partner = kz * 2 + q
    zup = lax.rem(kz + 1, K) * 2 + p
    zdown = lax.rem(kz + K - 1, K) * 2 + p
    xup = lax.rem(mx + 1, nx)
    xdown = lax.rem(mx + nx - 1, nx)

    def load(src, dst, i):
        copy = pltpu.make_async_copy(src, dst, ls.at[i])
        copy.start()
        return copy

    away = [load(start_h.at[q * S + c], start.at[c], c) for c in range(S)]
    level_load = load(dis_h, dis, 2 * S)
    kept = [load(start_h.at[p * S + c], start.at[S + c], S + c) for c in range(S)]
    ritz_load = load(ritz_h, ritz, 2 * S + 1)
    barrier = pltpu.get_barrier_semaphore()

    def greet(dev):
        pl.semaphore_signal(barrier, inc=1, device_id=dev, device_id_type=MESH)

    def in_plane(o):
        t = lax.rem(g + o, ng)
        return t, (cut, t // 2, kz * 2 + lax.rem(t, 2))

    def in_line(o):
        t = lax.rem(kz + o, K)
        return t, (cut, mx, t * 2 + p)

    for o in range(1, ng):
        greet(in_plane(o)[1])
    for o in range(1, K):
        greet(in_line(o)[1])
    cup = (lax.rem(cut + 1, nc), mx, my)
    cdown = (lax.rem(cut + nc - 1, nc), mx, my)
    greet(cup)
    greet(cdown)

    lo = H + Y * p
    for c in range(NC):
        if c % CH == 0:
            away[c // CH].wait()
        for x in range(X):
            for r in range(Y):
                T[c, x, r] = start[c // CH, pl.ds((c % CH) * W * J + x * Y + r, W, stride=J), :]
    level_load.wait()
    for x in range(X):
        for r in range(Y):
            row = dis[pl.ds(x * Y + r, 1), :].astype(jnp.float32)
            row = 16.5 * (row / jnp.float32(LEVELS - 1) - 0.5)
            O[H + x, lo + r] = jnp.broadcast_to(row, (8, NZ))
    pl.semaphore_wait(barrier, ng + K)

    pending = []

    def send(src, dst, ss, rs_, dev):
        copy = pltpu.make_async_remote_copy(
            src_ref=src, dst_ref=dst, send_sem=ss, recv_sem=rs_, device_id=dev, device_id_type=MESH)
        copy.start()
        pending.append(copy)

    def arrived(dst, rs_):
        pltpu.make_async_remote_copy(
            src_ref=dst, dst_ref=dst, send_sem=rs_, recv_sem=rs_,
            device_id=(cut, mx, partner), device_id_type=MESH).wait_recv()

    fields = [(NC, O)] + [(c, E.at[c]) for c in range(NC)]
    xi = pl.ds(H, X)
    xy = (cut, mx, partner)

    def row_block(at):
        return pl.ds(at, Y)

    def send_rows(c, buf, half):
        up = half
        target = jnp.where(up == 1, zup, zdown)
        dst_row = jnp.where(up == 1, 0, H + R)
        side = 1 - up
        send(buf.at[xi, row_block(H + Y * half)], buf.at[xi, row_block(dst_row)],
             hs.at[c, 1 + side], hr.at[c, 1 + side], (cut, mx, target))

    for c, buf in fields:
        src = buf.at[xi, row_block(lo)] if c == NC else T.at[c]
        send(src, buf.at[xi, row_block(lo)], hs.at[c, 0], hr.at[c, 0], xy)
    for c in range(NC):
        if c % CH == 0:
            kept[c // CH].wait()
        for x in range(X):
            for r in range(Y):
                E[c, H + x, lo + r] = start[S + c // CH, pl.ds((c % CH) * W * J + x * Y + r, W, stride=J), :]
    for c, buf in fields[:2]:
        send_rows(c, buf, p)
    ritz_load.wait()
    for s in range(count):
        for x in range(X):
            for r in range(Y):
                RA[s + 1, x, r] = ritz[s, pl.ds(x * Y + r, NR, stride=J), :]

    own = pl.ds(H, R)
    for c, buf in fields:
        arrived(buf.at[xi, row_block(H + Y * q)], hr.at[c, 0])
        send_rows(c, buf, q)
        if c < NC - 1:
            send_rows(c + 1, fields[c + 2][1], p)
        send(buf.at[pl.ds(X, H), own], buf.at[pl.ds(0, H), own], hs.at[c, 3], hr.at[c, 3], (cut, xup, my))
        send(buf.at[pl.ds(H, H), own], buf.at[pl.ds(H + X, H), own], hs.at[c, 4], hr.at[c, 4], (cut, xdown, my))

    send(RA.at[count], RA.at[0], rs.at[0], rr.at[0], cup)
    send(RA.at[1], RA.at[count + 1], rs.at[1], rr.at[1], cdown)

    def point(src, c, x, r, centre):
        v = src(x, r)
        beside = src(x + 1, r) + src(x - 1, r)
        beside = beside + src(x, r + 1) + src(x, r - 1)
        beside = beside + pltpu.roll(v, 1, 1) + pltpu.roll(v, NZ - 1, 1)
        level = O[x, r] - centre
        level = jnp.concatenate([level] * (W // 8), 0)
        return (level * v - beside) * 0.0625

    for c, buf in fields:
        for side, row in ((0, 0), (1, H + R)):
            arrived(buf.at[xi, row_block(row)], hr.at[c, 1 + side])
        for side, row in ((0, 1), (1, H + R)):
            send(buf.at[H + X - 1, row], buf.at[1, row], hs.at[c, 5 + 2 * side], hr.at[c, 5 + 2 * side], (cut, xup, my))
            send(buf.at[H, row], buf.at[H + X, row], hs.at[c, 6 + 2 * side], hr.at[c, 6 + 2 * side], (cut, xdown, my))
        arrived(buf.at[pl.ds(0, H), own], hr.at[c, 3])
        arrived(buf.at[pl.ds(H + X, H), own], hr.at[c, 4])
        for side, row in ((0, 1), (1, H + R)):
            arrived(buf.at[1, row], hr.at[c, 5 + 2 * side])
            arrived(buf.at[H + X, row], hr.at[c, 6 + 2 * side])
        if c == NC:
            continue
        s = p * S + c // CH
        part = pl.ds((c % CH) * W, W)
        centre = (bnd[0, s] + bnd[1, s]) / 2.0

        def from_e(x, r, c=c):
            return E[c, x, r]

        def from_u(x, r):
            return U[x, r]

        for x in (1, H + X):
            for r in range(H, H + R):
                U[x, r] = point(from_e, c, x, r, centre)

        def first(i, carry, c=c, centre=centre):
            for r in range(1, H + R + 1):
                U[H + i, r] = point(from_e, c, H + i, r, centre)
            return carry

        lax.fori_loop(0, X, first, 0)

        def second(i, carry, c=c, s=s, centre=centre, part=part):
            for r in range(Y):
                a = H + Y * p + r
                FA[s, i, r, part] = 2.0 * point(from_u, c, H + i, a, centre) - E[c, H + i, a]
                b = H + Y * q + r
                FT[c, i, r] = 2.0 * point(from_u, c, H + i, b, centre) - E[c, H + i, b]
            return carry

        lax.fori_loop(0, X, second, 0)
        send(FT.at[c], FA.at[s, :, :, part], fs.at[c], fr.at[c], xy)

    arrived(RA.at[0], rr.at[0])
    arrived(RA.at[count + 1], rr.at[1])

    @pl.when(cut == 0)
    def _():
        RA[0] = jnp.zeros((X, Y, NR, NZ), jnp.float32)

    @pl.when(cut == nc - 1)
    def _():
        RA[count + 1] = jnp.zeros((X, Y, NR, NZ), jnp.float32)

    for c in range(NC):
        arrived(FA.at[q * S + c // CH, :, :, pl.ds((c % CH) * W, W)], fr.at[c])

    contract = (((1,), (1,)), ((), ()))
    ACC[...] = jnp.zeros(ACC.shape, jnp.float32)

    def grams(i, carry):
        z = [jnp.concatenate([FA[s, i, r] for s in range(count)] + [RA[t, i, r] for t in range(count + 2)], 0)
             for r in range(Y)]
        z = jnp.concatenate(z, 1)
        ACC[...] += lax.dot_general(z, z, contract, precision=HP, preferred_element_type=jnp.float32)
        return carry

    lax.fori_loop(0, X, grams, 0)

    NL = ACC.shape[1]
    base = count * NV
    lane = lax.broadcasted_iota(jnp.int32, (8, NL), 1)

    def masked(row, first, width):
        keep = jnp.logical_and(lane >= first, lane < first + width)
        return jnp.where(keep, ACC[pl.ds(row, 8), :], 0.0)

    packed = []
    for b in range(NV // 8):
        acc = jnp.zeros((8, NL), jnp.float32)
        for s in range(count):
            acc = acc + masked(s * NV + b * 8, s * NV, NV)
        if b == 0:
            for t in range(count + 2):
                acc = acc + masked(base + t * NR, base + t * NR, NR)
        if b == 1:
            for s in range(count):
                acc = acc + masked(base + s * NR, base + (s + 2) * NR, NR)
        if b == 2:
            for s in range(count):
                acc = acc + masked(base + (s + 2) * NR, base + s * NR, NR)
        packed.append(acc)
    for b in range(2):
        acc = jnp.zeros((8, NL), jnp.float32)
        for s in range(count):
            acc = acc + masked(base + (s + 2 * b) * NR, s * NV, NV)
        packed.append(acc)
    halves = NL // 128
    used = len(packed) * halves
    for i in range(tiles):
        if i < used:
            h = i % halves
            PK[i] = packed[i // halves][:, h * 128:(h + 1) * 128]
        else:
            PK[i] = jnp.zeros((8, 128), jnp.float32)

    RX[g] = PK[pl.ds(g * tg, tg)]
    for o in range(1, ng):
        t, dev = in_plane(o)
        send(PK.at[pl.ds(t * tg, tg)], RX.at[g], xs.at[o], xr.at[g], dev)
    for o in range(1, ng):
        t, _ = in_plane(o)
        arrived(RX.at[t], xr.at[t])
    mine = RX[0]
    for t in range(1, ng):
        mine = mine + RX[t]
    RZ[kz] = mine
    SM[...] = mine
    for o in range(1, K):
        t, dev = in_line(o)
        send(SM, RZ.at[kz], zs.at[o], zr.at[kz], dev)
    for o in range(1, K):
        t, _ = in_line(o)
        arrived(RZ.at[t], zr.at[t])
    mine = RZ[0]
    for t in range(1, K):
        mine = mine + RZ[t]
    AL[g] = mine
    for o in range(1, ng):
        t, dev = in_plane(o)
        send(AL.at[g], AL.at[g], gs.at[o], gr.at[g], dev)
    for o in range(1, ng):
        t, _ = in_plane(o)
        arrived(AL.at[t], gr.at[t])

    def tile(row, first):
        i = row * halves + first // 128
        value = AL[i // tg, i % tg] * (1.0 / total)
        shift = first % 128
        return pltpu.roll(value, 128 - shift, 1) if shift else value

    l8 = lax.broadcasted_iota(jnp.int32, (8, 128), 1)
    l32 = lax.broadcasted_iota(jnp.int32, (NV, 128), 1)
    r32 = lax.broadcasted_iota(jnp.int32, (NV, 128), 0)
    eye = jnp.where(l32 == r32 + NV, 1.0, 0.0)
    e16r = lax.broadcasted_iota(jnp.int32, (2 * NR, 128), 0)
    e16l = lax.broadcasted_iota(jnp.int32, (2 * NR, 128), 1)
    corrs, mats = [], []
    for s in range(count):
        corr = jnp.concatenate([tile(NV // 8 + b, s * NV) for b in range(2)], 0)[:, :NV]
        corrs.append(corr)
        cor[s] = corr
        a00 = tile(0, base + s * NR)
        a11 = pltpu.roll(tile(0, base + (s + 2) * NR), NR, 1)
        a01 = pltpu.roll(tile(1, base + (s + 2) * NR), NR, 1)
        a10 = tile(2, base + s * NR)
        b = jnp.concatenate([jnp.where(l8 < NR, a00, a01), jnp.where(l8 < NR, a10, a11)], 0)
        b = jnp.where(e16r == e16l, 2.0, 0.0) - b
        b = b[:, :2 * NR]
        bc = lax.dot_general(b, corr, (((1,), (0,)), ((), ())), precision=HP, preferred_element_type=jnp.float32)
        sub = lax.dot_general(corr, bc, (((0,), (0,)), ((), ())), precision=HP, preferred_element_type=jnp.float32)
        ff = jnp.concatenate([tile(b_, s * NV) for b_ in range(NV // 8)], 0)
        sub = jnp.concatenate([sub, jnp.zeros((NV, 128 - NV), jnp.float32)], 1)
        mats.append(jnp.where(l32 < NV, ff - sub, eye)[None])
    M = jnp.concatenate(mats, 0)
    rows = lax.broadcasted_iota(jnp.int32, (1, NV, 1), 1)
    for k in range(NV):
        pivot = M[:, k:k + 1, :]
        inv = 1.0 / pivot[:, :, k:k + 1]
        f = jnp.where(rows > k, M[:, :, k:k + 1] * inv, 0.0)
        M = M - f * pivot
    diag = jnp.sum(jnp.where(l32[None] == r32[None], M, 0.0), axis=2, keepdims=True)
    M = M * (1.0 / jnp.sqrt(diag))
    ident = jnp.where(l32 == r32, 1.0, 0.0)[:, :NV]
    for s in range(count):
        linv = pltpu.roll(M[s], 128 - NV, 1)[:, :NV]
        full = jnp.concatenate([ident, -corrs[s]], 0)
        LM[s] = lax.dot_general(linv, full, contract, precision=HP, preferred_element_type=jnp.float32)

    def finish(s, carry):
        left = LM[s]
        for x in range(X):
            z = [jnp.concatenate([FA[s, x, r], RA[s, x, r], RA[s + 2, x, r]], 0) for r in range(Y)]
            z = jnp.concatenate(z, 1)
            o = lax.dot_general(left, z, (((1,), (0,)), ((), ())), precision=HP, preferred_element_type=jnp.float32)
            for r in range(Y):
                out[s, pl.ds(x * Y + r, NV, stride=J), :] = o[:, r * NZ:(r + 1) * NZ]
        return carry

    lax.fori_loop(0, count, finish, 0)
    for copy in pending:
        copy.wait_send()


def on_device(disorder, slice_bounds, start, ritz):
    nc, nx, ny = (lax.axis_size(a) for a in ("cuts", "lx", "ly"))
    count, NV, X, Y, NZ = start.shape
    NR = ritz.shape[1]
    J = X * Y
    S, R, K, ng = count // 2, 2 * Y, ny // 2, nx * 2
    CH = 1
    NC, W = S * CH, NV // CH
    NL = count * NV + (count + 2) * NR
    tg = -(-((NV + 2 * NR) // 8 * (NL // 128)) // ng)
    f32 = jnp.float32
    V = pltpu.VMEM
    D = pltpu.SemaphoreType.DMA
    dims = (nc, nx, ny, count, NV, NR, X, Y, NZ)
    vm = pl.BlockSpec(memory_space=pltpu.VMEM)
    hbm = pl.BlockSpec(memory_space=pl.ANY)
    block, corr = pl.pallas_call(
        functools.partial(kernel, dims),
        out_shape=(jax.ShapeDtypeStruct((count, NV * J, NZ), f32),
                   jax.ShapeDtypeStruct((count, 2 * NR, NV), f32)),
        in_specs=[hbm, pl.BlockSpec(memory_space=pltpu.SMEM), hbm, hbm],
        out_specs=(vm, vm),
        scratch_shapes=[
            V((J, NZ), jnp.int32),
            V((count, NV * J, NZ), f32),
            V((count, NR * J, NZ), f32),
            D((2 * S + 2,)),
            V((NC, X + 2 * H, R + 2 * H, W, NZ), f32),
            V((NC, X, Y, W, NZ), f32),
            V((X + 2 * H, R + 2 * H, 8, NZ), f32),
            V((X + 2 * H, R + 2 * H, W, NZ), f32),
            V((count, X, Y, NV, NZ), f32),
            V((NC, X, Y, W, NZ), f32),
            V((count + 2, X, Y, NR, NZ), f32),
            V((NL, NL), f32),
            V((count, NV, NV + 2 * NR), f32),
            V((ng * tg, 8, 128), f32),
            V((ng, tg, 8, 128), f32),
            V((K, tg, 8, 128), f32),
            V((tg, 8, 128), f32),
            V((ng, tg, 8, 128), f32),
            D((NC + 1, 9)), D((NC + 1, 9)), D((NC,)), D((NC,)), D((2,)), D((2,)),
            D((ng,)), D((ng,)), D((K,)), D((K,)), D((ng,)), D((ng,)),
        ],
        compiler_params=pltpu.CompilerParams(collective_id=0, has_side_effects=True, vmem_limit_bytes=67043328),
    )(disorder.reshape(J, NZ), slice_bounds.T, start.reshape(count, NV * J, NZ), ritz.reshape(count, NR * J, NZ))
    return (block.reshape(start.shape), corr)


def solution(mesh):
    in_specs = (
        P("lx", "ly", None),
        P("cuts", None),
        P("cuts", None, "lx", "ly", None),
        P("cuts", None, "lx", "ly", None),
    )
    out_specs = (P("cuts", None, "lx", "ly", None), P("cuts", None, None))
    return jax.shard_map(
        on_device, mesh=mesh, in_specs=in_specs, out_specs=out_specs, check_vma=False
    )
```
